32 devices in a mesh: chip: 8 (over z, x), cores: 4 (over y, core).
Axes of the slice: x: 2, y: 2, z: 4, core: 2. Of those that a mesh axis runs over, the one named last changes fastest.
Arguments:
- start_offset: float32 [1024, 512], P(('chip', 'cores')), may hold values from -4 to 4
- chars: float32 [1024, 6, 512], P(('chip', 'cores')), may hold values from -3 to 3
- share_rel: float32 [1024, 512], P(('chip', 'cores')), may hold values from -2.5 to 2.5
- draws: float32 [1024, 6, 768], P(('chip', 'cores')), may hold values from -3 to 3
- sigma: float32 [6], replicated, may hold values from 0.1 to 0.8
- counts: int32 [1024], P(('chip', 'cores')), may hold values from 8 to 512, as said below
- converged: int32 [1024], P(('chip', 'cores')), may hold values from 0 to 1, as said below
- destination: int32 [1024], P(('chip', 'cores')), may hold values from -1 to 383, as said below
Outputs:
- delta: float32 [1024, 512], P(('chip', 'cores'))
- work_delta: float32 [384, 512], P(('chip', 'cores'))
- step_norm: float32 [], replicated
The draws below stay inside these ranges and needn't reach their ends.
Inputs may be any that keep to these rules, and one draw needn't show every extreme that they name: `counts`: on every device one market has exactly 512 products. On every device between 4 and 20 markets have converged 0. destination is -1 exactly where converged is 1; otherwise it is v * 12 + s with s < 12 and v a device (numbered chip-major over chip and cores) with the same cores index as the market's own device. Every device's 12 slots are each named exactly once. At most 3 markets of one device name slots of one other device, and some pair reaches that number.
All inputs are finite; a program needn't handle non-finite values.
Results may differ from the reference program's by a relative error of at most 0.0003.
Values sent between devices are 32-bit elements; how exact they have to be, the bound alone decides.
A program may use at most 64 MiB of HBM per device.

```python
import math
import jax
import jax.numpy as jnp
from jax import lax

LOCAL_TRADE_ZONE = 32
PMAX = 512
K = 6
R = 768
TAIL_ITERS = 4
MARKETS = 1024
SLOTS = 12
N_CHIP = 8
N_CORES = 4
DEVICES = 32


def integer_plan(key):
    devices = N_CHIP * N_CORES
    markets = LOCAL_TRADE_ZONE * devices
    order = jnp.arange(markets, dtype=jnp.int32)
    device_of = order // LOCAL_TRADE_ZONE
    local_of = order % LOCAL_TRADE_ZONE
    chip_of = device_of // N_CORES
    core_of = device_of % N_CORES
    counts = jax.random.randint(jax.random.fold_in(key, 11), (markets,), 8, PMAX + 1, dtype=jnp.int32)
    widest = jax.random.randint(jax.random.fold_in(key, 12), (devices,), 0, LOCAL_TRADE_ZONE, dtype=jnp.int32)
    counts = jnp.where(local_of == widest[device_of], PMAX, counts).astype(jnp.int32)
    chip_line = jnp.arange(N_CHIP, dtype=jnp.int32)
    even_allotment = LOCAL_TRADE_ZONE // 8 + chip_line * (LOCAL_TRADE_ZONE // 2) // (N_CHIP - 1)
    leftover_regions = N_CHIP * (3 * LOCAL_TRADE_ZONE // 8) - jnp.sum(even_allotment)
    scores = jax.random.randint(jax.random.fold_in(key, 13), (N_CORES, N_CHIP - 1), 0, 2 ** 20, dtype=jnp.int32) * N_CHIP + chip_line[None, :N_CHIP - 1]
    accelerator_indices = jnp.argsort(jnp.argsort(scores, axis=1, stable=True), axis=1, stable=True)
    extra_allotment = (accelerator_indices < leftover_regions).astype(jnp.int32)
    extra_allotment = jnp.concatenate([extra_allotment, jnp.zeros((N_CORES, 1), jnp.int32)], axis=1)
    awaiting_regions = even_allotment[None, :] + extra_allotment
    u_of = awaiting_regions[core_of, chip_of]
    local_scores = jax.random.randint(jax.random.fold_in(key, 14), (devices, LOCAL_TRADE_ZONE), 0, 2 ** 20, dtype=jnp.int32) * LOCAL_TRADE_ZONE + jnp.arange(LOCAL_TRADE_ZONE, dtype=jnp.int32)[None, :]
    local_rank = jnp.argsort(jnp.argsort(local_scores, axis=1, stable=True), axis=1, stable=True).reshape(markets)
    moving = local_rank < u_of
    converged = jnp.where(moving, 0, 1).astype(jnp.int32)
    position = jnp.cumsum(moving.astype(jnp.int32).reshape(devices, LOCAL_TRADE_ZONE), axis=1).reshape(markets) - 1
    before = jnp.cumsum(awaiting_regions, axis=1) - awaiting_regions
    sequence = before[core_of, chip_of] + position
    shift = jax.random.randint(jax.random.fold_in(key, 15), (N_CORES,), 0, N_CHIP, dtype=jnp.int32)
    dest_chip = (sequence + shift[core_of]) % N_CHIP
    dest_slot = sequence // N_CHIP
    destination = jnp.where(moving, (dest_chip * N_CORES + core_of) * SLOTS + dest_slot, -1).astype(jnp.int32)
    return (counts, converged, destination)


def draw_counts(key, part):
    return integer_plan(key)[0]


def draw_converged(key, part):
    return integer_plan(key)[1]


def draw_destination(key, part):
    return integer_plan(key)[2]


def block_levels(key, dims, cuts, low, largest):
    def one(axis_at, parts):
        steps = jax.random.uniform(jax.random.fold_in(jax.random.fold_in(key, 6), axis_at), (parts,), jnp.float32, low / len(cuts), largest / len(cuts))
        return jnp.repeat(jnp.exp(steps), dims[axis_at] // parts).reshape((-1,) + (1,) * (len(dims) - axis_at - 1))

    gain = one(*cuts[0])
    for cut in cuts[1:]:
        gain = gain * one(*cut)
    return gain


def bell_draw(stream_key, extent, width, limit, pieces=(), kind=jnp.bfloat16):
    entries = jax.random.normal(stream_key, extent, jnp.float32) * width
    if len(pieces) > 0:
        entries = block_levels(stream_key, extent, pieces, -0.22, 0.18) * entries
    return jnp.clip(entries, min=-limit, max=limit).astype(kind)


def setup_inputs(seed: int = 0) -> dict:
    seeds = jax.random.split(jax.random.key(seed), 9)
    return {
        "start_offset": bell_draw(seeds[0], (MARKETS, PMAX), 1.0, 4.0, ((0, 32),), jnp.float32),
        "chars": bell_draw(seeds[1], (MARKETS, K, PMAX), 1.0, 3.0, ((0, 32),), jnp.float32),
        "share_rel": bell_draw(seeds[2], (MARKETS, PMAX), 0.5, 2.5, ((0, 32),), jnp.float32),
        "draws": bell_draw(seeds[3], (MARKETS, K, R), 1.0, 3.0, ((0, 32),), jnp.float32),
        "sigma": jnp.clip(jnp.exp(jax.random.uniform(seeds[4], (K,), jnp.float32, math.log(0.1), math.log(0.8))), 0.1, 0.8),
        "counts": draw_counts(jax.random.fold_in(seeds[8], 71), 0),
        "converged": draw_converged(jax.random.fold_in(seeds[8], 71), 0),
        "destination": draw_destination(jax.random.fold_in(seeds[8], 71), 0),
    }


def shock_table(features, market_draws, live_rows, coef_scale):
    spread = jnp.einsum('kj,kr->jr', features * coef_scale[:, None], market_draws, precision=lax.Precision.HIGHEST)
    return jnp.exp(spread) * live_rows[:, None]

def contract(deltas, table, log_share, live_rows):
    utility = jnp.exp(deltas)[:, None] * table
    inside = lax.optimization_barrier(jnp.sum(utility, axis=0))
    predicted = lax.optimization_barrier(jnp.mean(utility / (1.0 + inside)[None, :], axis=1))
    updated = deltas + log_share - jnp.log(jnp.where(live_rows > 0, predicted, 1.0))
    return updated * live_rows

def reference(start_offset, chars, share_rel, draws, sigma, counts, converged, destination):
    positions = jnp.arange(PMAX, dtype=jnp.int32)
    live_mask = (positions[None, :] < counts[:, None]).astype(start_offset.dtype)
    log_obs = share_rel - jnp.log(counts.astype(share_rel.dtype))[:, None] - 1.5
    initial = (log_obs + start_offset) * live_mask

    def market(packed):
        deltas, features, log_share, market_draws, live_rows = packed
        table = shock_table(features, market_draws, live_rows, sigma)
        initial_update = contract(deltas, table, log_share, live_rows)
        second = contract(initial_update, table, log_share, live_rows)
        latest = second
        for step in range(TAIL_ITERS):
            latest = contract(latest, table, log_share, live_rows)
        return (second, latest)
    second, final_step = lax.map(market, (initial, chars, log_obs, draws, live_mask))
    keep_mask = (converged == 1)[:, None]
    deltas = jnp.where(keep_mask, second, final_step)
    change = jnp.sum(jnp.where(keep_mask, 0.0, (final_step - second) ** 2))
    active = jnp.sum(jnp.where(converged == 1, 0, counts)).astype(jnp.int32)
    step_norm = jnp.sqrt(change / active.astype(change.dtype))
    slot_index = jnp.where(converged == 1, DEVICES * SLOTS, destination).astype(jnp.int32)
    work_delta = jnp.zeros((DEVICES * SLOTS, PMAX), final_step.dtype).at[slot_index].set(final_step, mode='drop')
    return (deltas, work_delta, step_norm)
```

```python
import functools
import math

import jax
import jax.numpy as jnp
from jax import lax
from jax.experimental import pallas as pl
from jax.experimental.pallas import tpu as pltpu
from jax.sharding import PartitionSpec as P

TAIL_ITERS = 4
LANES = 128
GROUP = 4
LIFT = 2.0**30
MESH = pl.DeviceIdType.MESH


def split_rows(row):
    wide = jnp.broadcast_to(row, (8, row.shape[1]))
    high = wide.astype(jnp.bfloat16).astype(jnp.float32)
    line = lax.broadcasted_iota(jnp.int32, wide.shape, 0)
    both = jnp.where(line == 0, high, jnp.where(line == 1, wide - high, 0.0))
    return both.astype(jnp.bfloat16)


def split_stack(block, order):
    pad = jnp.zeros((8 - block.shape[0], block.shape[1]), jnp.float32)
    full = jnp.concatenate([block, pad], axis=0)
    high = full.astype(jnp.bfloat16).astype(jnp.float32)
    parts = (high, full - high)
    return jnp.concatenate([parts[i] for i in order], axis=0).astype(jnp.bfloat16)


def market_kernel(
    slots, cores, order_ref, counts_ref, conv_ref, dest_ref, sigma_ref, start_ref, share_ref,
    chars_ref, draws_ref, delta_ref, send_ref, table_ref, change_ref, used_ref,
):
    markets, width = start_ref.shape
    factors = chars_ref.shape[1]
    consumers = draws_ref.shape[2]
    chips, rows = send_ref.shape[0], send_ref.shape[1]
    pair_room = rows - 1
    group = table_ref.shape[0]
    send_ref[...] = jnp.full(send_ref.shape, float(slots), jnp.float32)
    change_ref[...] = jnp.zeros_like(change_ref)
    for c in range(chips):
        used_ref[c] = 0
    kline = lax.broadcasted_iota(jnp.int32, (factors, 1), 0)
    scale = jnp.zeros((factors, 1), jnp.float32)
    for k in range(factors):
        scale = jnp.where(kline == k, sigma_ref[k] * math.log2(math.e), scale)

    def run(which, blocks, any_moving):
        span = blocks * LANES
        lane = lax.broadcasted_iota(jnp.int32, (1, span), 1)
        live, observed, lifted, start = [], [], [], []
        for g in range(group):
            m = which[g]
            n = counts_ref[m]
            alive = lane < n
            log_obs = (
                share_ref[pl.ds(m, 1), :][:, :span]
                - jnp.log(jnp.full((1, span), n, jnp.int32).astype(jnp.float32))
                - 1.5
            )
            live.append(alive)
            observed.append(log_obs)
            lifted.append(jnp.exp(log_obs) * LIFT)
            start.append(jnp.where(alive, jnp.exp(log_obs + start_ref[pl.ds(m, 1), :][:, :span]), 0.0))
            right = split_stack(draws_ref[m], (0, 1, 0, 1))
            for b in range(blocks):
                left = split_stack(chars_ref[m, :, b * LANES:(b + 1) * LANES] * scale, (0, 0, 1, 1))
                spread = lax.dot_general(
                    left, right, (((0,), (0,)), ((), ())), preferred_element_type=jnp.float32
                )
                table_ref[g, b * LANES:(b + 1) * LANES, :] = jnp.exp2(spread).astype(jnp.bfloat16)

        def contract(weights):
            means = []
            for g in range(group):
                table = table_ref[g, :span, :]
                inside = jnp.dot(split_rows(weights[g]), table, preferred_element_type=jnp.float32)
                inside = jnp.sum(inside, axis=0, keepdims=True)
                share = (LIFT / consumers) / (1.0 + inside)
                mean = lax.dot_general(
                    split_rows(share), table, (((1,), (1,)), ((), ())),
                    preferred_element_type=jnp.float32,
                )
                means.append(jnp.sum(mean, axis=0, keepdims=True))
            return means

        def step(_, means):
            return tuple(contract([
                jnp.where(live[g], lifted[g] / means[g], 0.0) for g in range(group)
            ]))

        first = tuple(contract(start))
        second = step(0, first)
        last = lax.fori_loop(0, jnp.where(any_moving, TAIL_ITERS, 0), step, second)
        for g in range(group):
            m = which[g]
            moving = conv_ref[m] == 0
            before = jnp.where(live[g], jnp.log(second[g]), 0.0)
            after = jnp.where(live[g], jnp.log(last[g]), 0.0)
            gap = jnp.where(moving, after - before, 0.0)
            change_ref[:, :span] += gap * gap
            base = observed[g] + math.log(LIFT)
            result = jnp.where(live[g], base - jnp.where(moving, after, before), 0.0)
            if span < width:
                result = jnp.concatenate([result, jnp.zeros((1, width - span), jnp.float32)], axis=1)
            delta_ref[pl.ds(m, 1), :] = result

            @pl.when(moving)
            def _():
                slot = dest_ref[m]
                chip = slot // slots // cores
                place = used_ref[chip]
                used_ref[chip] = place + 1
                tag = jnp.full((1, LANES), slot % slots, jnp.int32).astype(jnp.float32)
                send_ref[chip, pl.ds(place, 1), :] = jnp.concatenate([result, tag], axis=1)

    def one_group(i, carry):
        which = [order_ref[i * group + g] for g in range(group)]
        most = counts_ref[which[0]]
        any_moving = conv_ref[which[0]] == 0
        for m in which[1:]:
            most = jnp.maximum(most, counts_ref[m])
            any_moving = jnp.logical_or(any_moving, conv_ref[m] == 0)
        need = (most + LANES - 1) // LANES
        for blocks in range(1, width // LANES + 1):
            pl.when(need == blocks)(functools.partial(run, which, blocks, any_moving))
        return carry

    lax.fori_loop(0, markets // group, one_group, 0)

    def add_active(m, total):
        return total + jnp.where(conv_ref[m] == 0, counts_ref[m], 0)

    active = lax.fori_loop(0, markets, add_active, 0)
    lane = lax.broadcasted_iota(jnp.int32, (1, width + LANES), 1)
    total = jnp.sum(change_ref[...])
    stats = jnp.where(
        lane < LANES, total, jnp.full(lane.shape, active, jnp.int32).astype(jnp.float32)
    )
    for c in range(chips):
        send_ref[c, pair_room:rows, :] = stats


def exchange_kernel(
    chips, cores, send_ref, work_ref, norm_ref, got_ref, part_ref, parts_ref,
    send_sem, recv_sem, core_send, core_recv,
):
    me = lax.axis_index("chip")
    core = lax.axis_index("cores")
    rows = send_ref.shape[1]
    slots, width = work_ref.shape
    barrier = pltpu.get_barrier_semaphore()
    for d in range(1, chips):
        pl.semaphore_signal(
            barrier, inc=1, device_id=(lax.rem(me + d, chips), core), device_id_type=MESH
        )
    for d in range(1, cores):
        pl.semaphore_signal(
            barrier, inc=1, device_id=(me, lax.rem(core + d, cores)), device_id_type=MESH
        )
    pl.semaphore_wait(barrier, chips + cores - 2)
    copies = []
    for d in range(1, chips):
        peer = lax.rem(me + d, chips)
        copy = pltpu.make_async_remote_copy(
            src_ref=send_ref.at[peer], dst_ref=got_ref.at[d],
            send_sem=send_sem.at[d], recv_sem=recv_sem.at[d],
            device_id=(peer, core), device_id_type=MESH,
        )
        copy.start()
        copies.append(copy)
    line = lax.broadcasted_iota(jnp.int32, (slots, width), 0).astype(jnp.float32)

    def place(out, block):
        for k in range(rows - 1):
            out = jnp.where(line == block[k:k + 1, width:width + 1], block[k:k + 1, :width], out)
        return out

    own = send_ref[me]
    got_ref[0] = own
    out = place(jnp.zeros((slots, width), jnp.float32), own)
    for d in range(1, chips):
        copies[d - 1].wait()
        block = got_ref[d]
        out = place(out, block)
    stats = jnp.zeros((1, 2 * LANES), jnp.float32)
    for c in range(chips):
        stats = stats + got_ref[lax.rem(me - c + chips, chips)][rows - 1:rows, :2 * LANES]
    part_ref[...] = jnp.broadcast_to(stats, part_ref.shape)
    copies = []
    for d in range(1, cores):
        copy = pltpu.make_async_remote_copy(
            src_ref=part_ref, dst_ref=parts_ref.at[d],
            send_sem=core_send.at[d], recv_sem=core_recv.at[d],
            device_id=(me, lax.rem(core + d, cores)), device_id_type=MESH,
        )
        copy.start()
        copies.append(copy)
    work_ref[...] = out
    for copy in copies:
        copy.wait()
    parts_ref[0] = part_ref[...]
    stats = parts_ref[lax.rem(core, cores)]
    for c in range(1, cores):
        stats = stats + parts_ref[lax.rem(core - c + cores, cores)]
    norm_ref[...] = jnp.sqrt(stats[:, :LANES] / stats[:, LANES:])


def local(start_offset, chars, share_rel, draws, sigma, counts, converged, destination):
    markets, width = start_offset.shape
    consumers = draws.shape[2]
    chips = lax.axis_size("chip")
    cores = lax.axis_size("cores")
    slots = 3 * markets // 8
    pair_room = (5 * markets // 8 + chips - 1) // chips
    group = math.gcd(GROUP, markets)
    key = jnp.where(converged == 0, 2 * width, 0) + counts
    line = jnp.arange(markets, dtype=jnp.int32)
    ahead = (key[None, :] > key[:, None]) | (
        (key[None, :] == key[:, None]) & (line[None, :] < line[:, None])
    )
    rank = jnp.sum(ahead.astype(jnp.int32), axis=1)
    order = jnp.sum(jnp.where(rank[None, :] == line[:, None], line[None, :], 0), axis=1)
    smem = pl.BlockSpec(memory_space=pltpu.SMEM)
    vmem = pl.BlockSpec(memory_space=pltpu.VMEM)
    delta, send = pl.pallas_call(
        functools.partial(market_kernel, slots, cores),
        out_shape=(
            jax.ShapeDtypeStruct((markets, width), jnp.float32),
            jax.ShapeDtypeStruct((chips, pair_room + 1, width + LANES), jnp.float32),
        ),
        in_specs=[smem] * 5 + [vmem] * 4,
        out_specs=(vmem, vmem),
        scratch_shapes=[
            pltpu.VMEM((group, width, consumers), jnp.bfloat16),
            pltpu.VMEM((1, width), jnp.float32),
            pltpu.SMEM((chips,), jnp.int32),
        ],
        name="markets",
    )(order, counts, converged, destination, sigma, start_offset, share_rel, chars, draws)
    work, norm = pl.pallas_call(
        functools.partial(exchange_kernel, chips, cores),
        out_shape=(
            jax.ShapeDtypeStruct((slots, width), jnp.float32),
            jax.ShapeDtypeStruct((8, LANES), jnp.float32),
        ),
        in_specs=[vmem],
        out_specs=(vmem, vmem),
        scratch_shapes=[
            pltpu.VMEM((chips, pair_room + 1, width + LANES), jnp.float32),
            pltpu.VMEM((8, 2 * LANES), jnp.float32),
            pltpu.VMEM((cores, 8, 2 * LANES), jnp.float32),
            pltpu.SemaphoreType.DMA((chips,)),
            pltpu.SemaphoreType.DMA((chips,)),
            pltpu.SemaphoreType.DMA((cores,)),
            pltpu.SemaphoreType.DMA((cores,)),
        ],
        compiler_params=pltpu.CompilerParams(collective_id=0, has_side_effects=True),
        name="exchange",
    )(send)
    return delta, work, norm[0, 0]


def solution(mesh):
    return jax.shard_map(
        local,
        mesh=mesh,
        in_specs=(
            P(("chip", "cores"), None),
            P(("chip", "cores"), None, None),
            P(("chip", "cores"), None),
            P(("chip", "cores"), None, None),
            P(),
            P(("chip", "cores")),
            P(("chip", "cores")),
            P(("chip", "cores")),
        ),
        out_specs=(P(("chip", "cores"), None), P(("chip", "cores"), None), P()),
        check_vma=False,
    )
```

```python
import functools
import math

import jax
import jax.numpy as jnp
from jax import lax
from jax.experimental import pallas as pl
from jax.experimental.pallas import tpu as pltpu
from jax.sharding import PartitionSpec as P

TAIL_ITERS = 4
LANES = 128
GROUP = 4
LIFT = 2.0**30
MESH = pl.DeviceIdType.MESH


def split_rows(row):
    wide = jnp.broadcast_to(row, (8, row.shape[1]))
    high = wide.astype(jnp.bfloat16).astype(jnp.float32)
    line = lax.broadcasted_iota(jnp.int32, wide.shape, 0)
    both = jnp.where(line == 0, high, jnp.where(line == 1, wide - high, 0.0))
    return both.astype(jnp.bfloat16)


def split_stack(block, order):
    pad = jnp.zeros((8 - block.shape[0], block.shape[1]), jnp.float32)
    full = jnp.concatenate([block, pad], axis=0)
    high = full.astype(jnp.bfloat16).astype(jnp.float32)
    parts = (high, full - high)
    return jnp.concatenate([parts[i] for i in order], axis=0).astype(jnp.bfloat16)


def market_kernel(
    slots, cores, counts_ref, conv_ref, dest_ref, sigma_ref, start_ref, share_ref,
    chars_ref, draws_ref, delta_ref, send_ref, table_ref, change_ref, used_ref, order_ref, bucket_ref,
):
    markets, width = start_ref.shape
    factors = chars_ref.shape[0]
    consumers = draws_ref.shape[2]
    chips, rows = send_ref.shape[0], send_ref.shape[1]
    pair_room = rows - 1
    group = table_ref.shape[0]
    send_ref[...] = jnp.full(send_ref.shape, float(slots), jnp.float32)
    change_ref[...] = jnp.zeros_like(change_ref)
    for c in range(chips):
        used_ref[c] = 0
    most_blocks = width // LANES
    buckets = 2 * most_blocks

    def bucket_of(m):
        need = (counts_ref[m] + LANES - 1) // LANES
        return jnp.where(conv_ref[m] == 0, 0, most_blocks) + most_blocks - need

    for c in range(buckets + 1):
        bucket_ref[c] = 0

    def tally(m, total):
        c = bucket_of(m)
        bucket_ref[c + 1] = bucket_ref[c + 1] + 1
        return total + jnp.where(conv_ref[m] == 0, counts_ref[m], 0)

    active = lax.fori_loop(0, markets, tally, 0)
    for c in range(1, buckets):
        bucket_ref[c] = bucket_ref[c] + bucket_ref[c - 1]

    def rank(m, carry):
        c = bucket_of(m)
        place = bucket_ref[c]
        bucket_ref[c] = place + 1
        order_ref[place] = m
        return carry

    lax.fori_loop(0, markets, rank, 0)
    kline = lax.broadcasted_iota(jnp.int32, (factors, 1), 0)
    scale = jnp.zeros((factors, 1), jnp.float32)
    for k in range(factors):
        scale = jnp.where(kline == k, sigma_ref[k] * math.log2(math.e), scale)

    def run(which, blocks, any_moving):
        span = blocks * LANES
        lane = lax.broadcasted_iota(jnp.int32, (1, span), 1)
        live, observed, lifted, start = [], [], [], []
        for g in range(group):
            m = which[g]
            n = counts_ref[m]
            alive = lane < n
            log_obs = (
                share_ref[pl.ds(m, 1), :][:, :span]
                - jnp.log(jnp.full((1, span), n, jnp.int32).astype(jnp.float32))
                - 1.5
            )
            live.append(alive)
            observed.append(log_obs)
            lifted.append(jnp.exp(log_obs) * LIFT)
            start.append(jnp.where(alive, jnp.exp(log_obs + start_ref[pl.ds(m, 1), :][:, :span]), 0.0))
            right = split_stack(draws_ref[:, m, :], (0, 1, 0, 1))
            scaled = split_stack(chars_ref[:, m, :] * scale, (0, 0, 1, 1))
            for b in range(blocks):
                left = scaled[:, b * LANES:(b + 1) * LANES]
                spread = lax.dot_general(
                    left, right, (((0,), (0,)), ((), ())), preferred_element_type=jnp.float32
                )
                table_ref[g, b * LANES:(b + 1) * LANES, :] = jnp.exp2(spread).astype(jnp.bfloat16)

        def contract(weights):
            means = []
            for g in range(group):
                table = table_ref[g, :span, :]
                inside = jnp.dot(split_rows(weights[g]), table, preferred_element_type=jnp.float32)
                inside = jnp.sum(inside, axis=0, keepdims=True)
                share = (LIFT / consumers) / (1.0 + inside)
                mean = lax.dot_general(
                    split_rows(share), table, (((1,), (1,)), ((), ())),
                    preferred_element_type=jnp.float32,
                )
                means.append(jnp.sum(mean, axis=0, keepdims=True))
            return means

        def step(_, means):
            return tuple(contract([
                jnp.where(live[g], lifted[g] / means[g], 0.0) for g in range(group)
            ]))

        first = tuple(contract(start))
        second = step(0, first)
        last = lax.fori_loop(0, jnp.where(any_moving, TAIL_ITERS, 0), step, second)
        for g in range(group):
            m = which[g]
            moving = conv_ref[m] == 0
            before = jnp.where(live[g], jnp.log(second[g]), 0.0)
            after = jnp.where(live[g], jnp.log(last[g]), 0.0)
            gap = jnp.where(moving, after - before, 0.0)
            change_ref[:, :span] += gap * gap
            base = observed[g] + math.log(LIFT)
            result = jnp.where(live[g], base - jnp.where(moving, after, before), 0.0)
            if span < width:
                result = jnp.concatenate([result, jnp.zeros((1, width - span), jnp.float32)], axis=1)
            delta_ref[pl.ds(m, 1), :] = result

            @pl.when(moving)
            def _():
                slot = dest_ref[m]
                chip = slot // slots // cores
                place = used_ref[chip]
                used_ref[chip] = place + 1
                tag = jnp.full((1, LANES), slot % slots, jnp.int32).astype(jnp.float32)
                send_ref[chip, pl.ds(place, 1), :] = jnp.concatenate([result, tag], axis=1)

    def one_group(i, carry):
        which = [order_ref[i * group + g] for g in range(group)]
        most = counts_ref[which[0]]
        any_moving = conv_ref[which[0]] == 0
        for m in which[1:]:
            most = jnp.maximum(most, counts_ref[m])
            any_moving = jnp.logical_or(any_moving, conv_ref[m] == 0)
        need = (most + LANES - 1) // LANES
        for blocks in range(1, width // LANES + 1):
            pl.when(need == blocks)(functools.partial(run, which, blocks, any_moving))
        return carry

    lax.fori_loop(0, markets // group, one_group, 0)

    lane = lax.broadcasted_iota(jnp.int32, (1, width + LANES), 1)
    total = jnp.sum(change_ref[...])
    stats = jnp.where(
        lane < LANES, total, jnp.full(lane.shape, active, jnp.int32).astype(jnp.float32)
    )
    for c in range(chips):
        send_ref[c, pair_room:rows, :] = stats


def exchange_kernel(
    chips, cores, send_ref, work_ref, norm_ref, got_ref, parts_ref,
    send_sem, recv_sem, part_send, part_recv,
):
    me = lax.axis_index("chip")
    core = lax.axis_index("cores")
    rows = send_ref.shape[1]
    slots, width = work_ref.shape
    others = [(d, e) for d in range(chips) for e in range(cores) if (d, e) != (0, 0)]

    def peer(d, e):
        return lax.rem(me + d, chips), lax.rem(core + e, cores)

    barrier = pltpu.get_barrier_semaphore()
    for d, e in others:
        pl.semaphore_signal(barrier, inc=1, device_id=peer(d, e), device_id_type=MESH)
    pl.semaphore_wait(barrier, len(others))
    blocks, sums = [], []
    for d in range(1, chips):
        copy = pltpu.make_async_remote_copy(
            src_ref=send_ref.at[peer(d, 0)[0]], dst_ref=got_ref.at[d],
            send_sem=send_sem.at[d], recv_sem=recv_sem.at[d],
            device_id=peer(d, 0), device_id_type=MESH,
        )
        copy.start()
        blocks.append(copy)
    for d, e in others:
        if e == 0:
            continue
        copy = pltpu.make_async_remote_copy(
            src_ref=send_ref.at[0, rows - 1:rows, :2 * LANES], dst_ref=parts_ref.at[d * cores + e],
            send_sem=part_send.at[d * cores + e], recv_sem=part_recv.at[d * cores + e],
            device_id=peer(d, e), device_id_type=MESH,
        )
        copy.start()
        sums.append(copy)
    line = lax.broadcasted_iota(jnp.int32, (slots, width), 0).astype(jnp.float32)

    def place(out, block):
        for k in range(rows - 1):
            out = jnp.where(line == block[k:k + 1, width:width + 1], block[k:k + 1, :width], out)
        return out

    own = send_ref[me]
    parts_ref[0] = own[rows - 1:rows, :2 * LANES]
    out = place(jnp.zeros((slots, width), jnp.float32), own)
    for d in range(1, chips):
        blocks[d - 1].wait()
        block = got_ref[d]
        parts_ref[d * cores] = block[rows - 1:rows, :2 * LANES]
        out = place(out, block)
    work_ref[...] = out
    for copy in sums:
        copy.wait()
    stats = jnp.zeros((1, 2 * LANES), jnp.float32)
    for c in range(chips):
        for e in range(cores):
            gap = lax.rem(me - c + chips, chips) * cores + lax.rem(core - e + cores, cores)
            stats = stats + parts_ref[gap]
    norm_ref[...] = jnp.sqrt(stats[:, :LANES] / stats[:, LANES:])


def local(start_offset, chars, share_rel, draws, sigma, counts, converged, destination):
    markets, width = start_offset.shape
    consumers = draws.shape[2]
    chips = lax.axis_size("chip")
    cores = lax.axis_size("cores")
    slots = 3 * markets // 8
    pair_room = (5 * markets // 8 + chips - 1) // chips
    group = math.gcd(GROUP, markets)
    smem = pl.BlockSpec(memory_space=pltpu.SMEM)
    vmem = pl.BlockSpec(memory_space=pltpu.VMEM)
    delta, send = pl.pallas_call(
        functools.partial(market_kernel, slots, cores),
        out_shape=(
            jax.ShapeDtypeStruct((markets, width), jnp.float32),
            jax.ShapeDtypeStruct((chips, pair_room + 1, width + LANES), jnp.float32),
        ),
        in_specs=[smem] * 4 + [vmem] * 4,
        out_specs=(vmem, vmem),
        scratch_shapes=[
            pltpu.VMEM((group, width, consumers), jnp.bfloat16),
            pltpu.VMEM((1, width), jnp.float32),
            pltpu.SMEM((chips,), jnp.int32),
            pltpu.SMEM((markets,), jnp.int32),
            pltpu.SMEM((2 * (width // LANES) + 1,), jnp.int32),
        ],
        name="markets",
    )(counts, converged, destination, sigma, start_offset, share_rel,
      jnp.transpose(chars, (1, 0, 2)), jnp.transpose(draws, (1, 0, 2)))
    work, norm = pl.pallas_call(
        functools.partial(exchange_kernel, chips, cores),
        out_shape=(
            jax.ShapeDtypeStruct((slots, width), jnp.float32),
            jax.ShapeDtypeStruct((1, LANES), jnp.float32),
        ),
        in_specs=[vmem],
        out_specs=(vmem, vmem),
        scratch_shapes=[
            pltpu.VMEM((chips, pair_room + 1, width + LANES), jnp.float32),
            pltpu.VMEM((chips * cores, 1, 2 * LANES), jnp.float32),
            pltpu.SemaphoreType.DMA((chips,)),
            pltpu.SemaphoreType.DMA((chips,)),
            pltpu.SemaphoreType.DMA((chips * cores,)),
            pltpu.SemaphoreType.DMA((chips * cores,)),
        ],
        compiler_params=pltpu.CompilerParams(collective_id=0, has_side_effects=True),
        name="exchange",
    )(send)
    return delta, work, norm[0, 0]


def solution(mesh):
    return jax.shard_map(
        local,
        mesh=mesh,
        in_specs=(
            P(("chip", "cores"), None),
            P(("chip", "cores"), None, None),
            P(("chip", "cores"), None),
            P(("chip", "cores"), None, None),
            P(),
            P(("chip", "cores")),
            P(("chip", "cores")),
            P(("chip", "cores")),
        ),
        out_specs=(P(("chip", "cores"), None), P(("chip", "cores"), None), P()),
        check_vma=False,
    )
```
